32 devices in a mesh: seq: 4 (over z), row: 8 (over y, x, core).
Axes of the slice: x: 2, y: 2, z: 4, core: 2. Of those that a mesh axis runs over, the one named last changes fastest.
Arguments:
- queries: bfloat16 [3, 128, 8192], P(None, 'row'), may hold values from -128 to 128
- prefix_keys: bfloat16 [6144, 512], P('seq'), may hold values from -6 to 6
- prefix_values: bfloat16 [6144, 512], P('seq'), may hold values from -6 to 6
- suffix_keys: bfloat16 [128, 256, 512], P('row', 'seq'), may hold values from -6 to 6
- suffix_values: bfloat16 [128, 256, 512], P('row', 'seq'), may hold values from -6 to 6
- new_keys: bfloat16 [3, 128, 512], P(None, 'row'), may hold values from -6 to 6
- new_values: bfloat16 [3, 128, 512], P(None, 'row'), may hold values from -6 to 6
- lengths: int32 [128], P('row'), may hold values from 16 to 256
- pair_of: int32 [128], replicated, may hold values from 0 to 127, as said below
- guidance: float32 [64], replicated, may hold values from 1 to 3
Outputs:
- guided: bfloat16 [3, 128, 8192], P(None, 'row', 'seq')
The draws below stay inside these ranges and needn't reach their ends.
Inputs may be any that keep to these rules, and one draw needn't show every extreme that they name: pair_of[pair_of[r]] = r; a row of the first half of the 128 rows is paired with a row of the second half, and pair_of[r] // 16 = (r // 16 + 128 / 32) mod (8).
All inputs are finite; a program needn't handle non-finite values.
Results may differ from the reference program's by a relative error of at most 0.014.
Values may be sent and summed in bfloat16 or wider, within the bound.
No kernel may reach another device: no remote copies, remote signals or barrier semaphores. Data moves between devices by JAX's collectives and lax.ppermute only.
A program may use at most 128 MiB of HBM per device.

```python
import jax
import jax.numpy as jnp
from jax import lax

H = 64
KVH = 4
HD = 128
STEPS = 3
ROW_DEV = 16
ROWS = 128
PREFIX = 6144
SUF = 256


def draw_queries(key, part):
    base = jnp.clip(jax.random.normal(key, (STEPS, ROWS, H * HD), jnp.float32), -6.0, 6.0)
    return base.astype(jnp.bfloat16)


def draw_pair_of(key, part):
    half = ROWS // 2
    blocks = half // ROW_DEV
    scores = jax.random.randint(jax.random.fold_in(key, 7), (blocks, ROW_DEV), 0, 1 << 20).astype(jnp.int32)
    scores = scores * ROW_DEV + jnp.arange(ROW_DEV, dtype=jnp.int32)[None, :]
    order = jnp.argsort(scores, axis=-1, stable=True).astype(jnp.int32)
    base = half + jnp.arange(blocks, dtype=jnp.int32)[:, None] * ROW_DEV
    upper = (base + order).reshape(half)
    lower = jnp.arange(half, dtype=jnp.int32)
    paired = jnp.zeros((ROWS,), jnp.int32).at[lower].set(upper).at[upper].set(lower)
    return paired


def with_ends(values, own_key, low, largest):
    place = [jax.random.randint(jax.random.fold_in(own_key, axis), (), 0, length) for axis, length in enumerate(values.shape)]
    main_axis = values.shape.index(max(values.shape))
    neighbour = place[:main_axis] + [(place[main_axis] + 1) % values.shape[main_axis]] + place[main_axis + 1:]
    return values.at[tuple(place)].set(low).at[tuple(neighbour)].set(largest)


def block_levels(stream_key, shape, pieces, least, high):
    def one(position, parts):
        steps = jax.random.uniform(jax.random.fold_in(jax.random.fold_in(stream_key, 6), position), (parts,), jnp.float32, least / len(pieces), high / len(pieces))
        return jnp.repeat(jnp.exp(steps), shape[position] // parts).reshape((-1,) + (1,) * (len(shape) - position - 1))

    loudness = one(*pieces[0])
    for cut in pieces[1:]:
        loudness = loudness * one(*cut)
    return loudness


def noise(rng, shape, scale, reach, cuts=(), kind=jnp.bfloat16):
    drawn = jax.random.normal(rng, shape, jnp.float32) * scale
    if len(cuts) > 0:
        drawn = block_levels(rng, shape, cuts, -0.22, 0.18) * drawn
    return jnp.clip(drawn, min=-reach, max=reach).astype(kind)


def setup_inputs(seed: int = 0) -> dict:
    seeds = jax.random.split(jax.random.key(seed), 11)
    queries = draw_queries(jax.random.fold_in(seeds[10], 71), 0)
    prefix_keys = noise(seeds[1], (PREFIX, KVH * HD), 1.0, 6.0, ((0, 4),))
    prefix_values = noise(seeds[2], (PREFIX, KVH * HD), 1.0, 6.0, ((0, 4),))
    suffix_keys = noise(seeds[3], (ROWS, SUF, KVH * HD), 1.0, 6.0, ((0, 8), (1, 4)))
    suffix_values = noise(seeds[4], (ROWS, SUF, KVH * HD), 1.0, 6.0, ((0, 8), (1, 4)))
    new_keys = noise(seeds[5], (STEPS, ROWS, KVH * HD), 1.0, 6.0, ((1, 8),))
    new_values = noise(seeds[6], (STEPS, ROWS, KVH * HD), 1.0, 6.0, ((1, 8),))
    lengths = with_ends(jax.random.randint(seeds[7], (ROWS,), SUF // 16, SUF + 1), jax.random.fold_in(seeds[7], 1), SUF // 16, SUF).astype(jnp.int32)
    pair_of = draw_pair_of(jax.random.fold_in(seeds[10], 71), 0)
    guidance = jnp.clip(jax.random.uniform(seeds[9], (H,), jnp.float32, 1.0, 3.0), 1.0, 3.0)
    return dict(queries=queries, prefix_keys=prefix_keys, prefix_values=prefix_values, suffix_keys=suffix_keys, suffix_values=suffix_values, new_keys=new_keys, new_values=new_values, lengths=lengths, pair_of=pair_of, guidance=guidance)


def reference(queries, prefix_keys, prefix_values, suffix_keys, suffix_values, new_keys, new_values, lengths, pair_of, guidance):
    group = H // KVH
    scale = HD ** (-0.5)
    pre_keys = prefix_keys.astype(jnp.float32).reshape(PREFIX, KVH, HD)
    pre_values = prefix_values.astype(jnp.float32).reshape(PREFIX, KVH, HD)
    step_index = jnp.arange(STEPS, dtype=jnp.int32)

    def one_row(index):
        query = queries[:, index].astype(jnp.float32).reshape(STEPS, KVH, group, HD)
        keys = jnp.concatenate([pre_keys, suffix_keys[index].astype(jnp.float32).reshape(SUF, KVH, HD), new_keys[:, index].astype(jnp.float32).reshape(STEPS, KVH, HD)], 0)
        values = jnp.concatenate([pre_values, suffix_values[index].astype(jnp.float32).reshape(SUF, KVH, HD), new_values[:, index].astype(jnp.float32).reshape(STEPS, KVH, HD)], 0)
        live_suffix = jnp.arange(SUF, dtype=jnp.int32) < lengths[index]
        shared = jnp.concatenate([jnp.ones((PREFIX,), bool), live_suffix])
        shared = jnp.broadcast_to(shared[None, :], (STEPS, PREFIX + SUF))
        causal = step_index[None, :] <= step_index[:, None]
        live = jnp.concatenate([shared, causal], 1)
        scores = jnp.einsum('tkgd,nkd->tkgn', query, keys) * scale
        scores = jnp.where(live[:, None, None, :], scores, -1e+30)
        top = lax.optimization_barrier(jnp.max(scores, -1, keepdims=True))
        weights = jnp.exp(scores - top)
        total = lax.optimization_barrier(jnp.sum(weights, -1))
        rounded = lax.optimization_barrier(weights.astype(jnp.bfloat16)).astype(jnp.float32)
        summed = jnp.einsum('tkgn,nkd->tkgd', rounded, values)
        return (summed / total[..., None]).reshape(STEPS, H, HD).astype(jnp.bfloat16)
    attention = lax.map(one_row, jnp.arange(ROWS, dtype=jnp.int32))
    rows = jnp.arange(ROWS, dtype=jnp.int32)
    cond = attention[jnp.minimum(rows, pair_of)].astype(jnp.float32)
    uncond = attention[jnp.maximum(rows, pair_of)].astype(jnp.float32)
    mix = uncond + guidance[None, None, :, None] * (cond - uncond)
    norm = jnp.sqrt(lax.optimization_barrier(jnp.mean(mix * mix, -1, keepdims=True)) + 1e-06)
    guided = (mix / norm).astype(jnp.bfloat16)
    return jnp.transpose(guided, (1, 0, 2, 3)).reshape(STEPS, ROWS, H * HD)
```

```python
import functools

import jax
import jax.numpy as jnp
from jax import lax
from jax.experimental import pallas as pl
from jax.experimental.pallas import tpu as pltpu
from jax.sharding import PartitionSpec as P

HD = 128
LOG2E = 1.4426950408889634
NEG = -1e30


def dot_nt(a, b):
    return lax.dot_general(a, b, (((1,), (1,)), ((), ())), preferred_element_type=jnp.float32)


def dot_nn(a, b):
    return lax.dot_general(a, b, (((1,), (0,)), ((), ())), preferred_element_type=jnp.float32)


def cdiv(a, b):
    return -(-a // b)


def lanes(x):
    return jnp.broadcast_to(x, (x.shape[0], HD))


def exp_weights(scores, top, scale):
    return jnp.exp2((scores - top) * scale)


def with_ones(values):
    return jnp.concatenate([values, jnp.ones_like(values)], axis=1)


def partial_kernel(
    own, chunk_rows, meta, lengths, q_ref, k_ref, v_ref, sk_ref, sv_ref, *rest
):
    if own:
        nk_ref, nv_ref, o_ref, lse_ref, qs, lses = rest
    else:
        o_ref, qs, lses = rest
    steps, row_dev, width = q_ref.shape
    share = width // HD
    per_row = steps * share
    rows = row_dev * per_row
    suf_dev = sk_ref.shape[1]
    scale = HD ** (-0.5) * LOG2E
    for t in range(steps):
        for g in range(share):
            qs[pl.ds(t * share + g, row_dev, stride=per_row), :] = q_ref[
                t, :, g * HD : (g + 1) * HD
            ].astype(jnp.float32)
    keys = k_ref[...]
    values = with_ones(v_ref[...])
    base = meta[2]
    if own:
        fresh = steps * row_dev
        new_keys = nk_ref[...].reshape(fresh, HD)
        new_values = with_ones(nv_ref[...].reshape(fresh, HD))
    for c in range(row_dev // chunk_rows):
        size = chunk_rows * per_row
        q = qs[c * size : (c + 1) * size, :].astype(jnp.bfloat16)
        pre = dot_nt(q, keys)
        top_pre = jnp.max(pre, axis=1, keepdims=True)
        sufs = []
        tops = []
        for p in range(chunk_rows // 2):
            r = c * chunk_rows + 2 * p
            sk = sk_ref[r : r + 2].reshape(2 * suf_dev, HD)
            s = dot_nt(q[p * 2 * per_row : (p + 1) * 2 * per_row], sk)
            lane = lax.broadcasted_iota(jnp.int32, s.shape, 1)
            second = lax.broadcasted_iota(jnp.int32, s.shape, 0) >= per_row
            live0 = jnp.clip(lengths[r] - base, 0, suf_dev)
            live1 = jnp.clip(lengths[r + 1] - base, 0, suf_dev)
            low = jnp.where(second, suf_dev, 0)
            high = jnp.where(second, suf_dev + live1, live0)
            s = jnp.where((lane >= low) & (lane < high), s, NEG)
            sufs.append(s)
            tops.append(jnp.max(s, axis=1, keepdims=True))
        top = jnp.maximum(top_pre, jnp.concatenate(tops, axis=0))
        if own:
            s = dot_nt(q, new_keys)
            row = lax.broadcasted_iota(jnp.int32, s.shape, 0)
            col = lax.broadcasted_iota(jnp.int32, s.shape, 1)
            same = (col % row_dev) == (c * chunk_rows + row // per_row)
            causal = (col // row_dev) <= ((row % per_row) // share)
            new = jnp.where(same & causal, s, NEG)
            top = jnp.maximum(top, jnp.max(new, axis=1, keepdims=True))
        w = exp_weights(pre, top, scale).astype(jnp.bfloat16)
        acc = dot_nn(w, values)
        parts = []
        for p in range(chunk_rows // 2):
            r = c * chunk_rows + 2 * p
            sv = with_ones(sv_ref[r : r + 2].reshape(2 * suf_dev, HD))
            part = slice(p * 2 * per_row, (p + 1) * 2 * per_row)
            w = exp_weights(sufs[p], top[part], scale).astype(jnp.bfloat16)
            parts.append(dot_nn(w, sv))
        acc = acc + jnp.concatenate(parts, axis=0)
        if own:
            w = exp_weights(new, top, scale).astype(jnp.bfloat16)
            acc = acc + dot_nn(w, new_values)
        total = acc[:, HD:]
        out = acc[:, :HD] / total
        lse = lanes(top * scale) + jnp.log2(total)
        o_ref[c * size : (c + 1) * size, :] = out.astype(o_ref.dtype)
        if own:
            lse_ref[c * size : (c + 1) * size, :] = lse
        else:
            lses[c * size : (c + 1) * size, :] = lse
    if not own:
        count = cdiv(rows, HD)
        eye = lax.broadcasted_iota(jnp.int32, (HD, HD), 0) == lax.broadcasted_iota(
            jnp.int32, (HD, HD), 1
        )
        if count * HD > rows:
            lses[rows:, :] = jnp.zeros((count * HD - rows, HD), jnp.float32)
        lines = [
            jnp.sum(jnp.where(eye, lses[b * HD : (b + 1) * HD, :], 0.0), axis=0, keepdims=True)
            for b in range(count)
        ]
        line = jnp.concatenate(lines, axis=0)
        high = line.astype(jnp.bfloat16)
        rest_1 = line - high.astype(jnp.float32)
        middle = rest_1.astype(jnp.bfloat16)
        low = (rest_1 - middle.astype(jnp.float32)).astype(jnp.bfloat16)
        stats = jnp.concatenate(
            [high.astype(jnp.float32), middle.astype(jnp.float32), low.astype(jnp.float32)], axis=0
        )
        pad = o_ref.shape[0] - rows - 3 * count
        if pad:
            stats = jnp.concatenate([stats, jnp.zeros((pad, HD), jnp.float32)], axis=0)
        o_ref[rows:, :] = stats.astype(jnp.bfloat16)


def combine_kernel(others, rows, *refs):
    received = refs[:others]
    o_ref, lse_ref, out_ref = refs[others:]
    count = cdiv(rows, HD)
    eye = lax.broadcasted_iota(jnp.int32, (HD, HD), 0) == lax.broadcasted_iota(
        jnp.int32, (HD, HD), 1
    )
    stats = []
    for ref in received:
        s = ref[rows:, :].astype(jnp.float32)
        stats.append(s[:count] + s[count : 2 * count] + s[2 * count : 3 * count])
    for b in range(count):
        size = min(HD, rows - b * HD)
        part = slice(b * HD, b * HD + size)
        all_lse = [lse_ref[part, :]]
        for s in stats:
            line = jnp.where(eye[:size], jnp.broadcast_to(s[b : b + 1], (size, HD)), 0.0)
            all_lse.append(lanes(jnp.sum(line, axis=1, keepdims=True)))
        top = functools.reduce(jnp.maximum, all_lse)
        weight = jnp.exp2(all_lse[0] - top)
        total = weight
        acc = o_ref[part, :] * weight
        for ref, lse in zip(received, all_lse[1:]):
            weight = jnp.exp2(lse - top)
            total = total + weight
            acc = acc + ref[part, :].astype(jnp.float32) * weight
        out_ref[part, :] = (acc / total).astype(jnp.bfloat16)


def mix_kernel(aligned, partner, lower, a_ref, b_ref, g_ref, out_ref, buf):
    steps, row_dev, width = out_ref.shape
    share = width // HD
    per_row = steps * share
    scales = g_ref[...]
    scales = jnp.concatenate([scales] * steps, axis=0)
    for r in range(row_dev):
        mine = a_ref[r * per_row : (r + 1) * per_row, :].astype(jnp.float32)
        start = pl.multiple_of(partner[r] * per_row, per_row) if aligned else r * per_row
        other = b_ref[pl.ds(start, per_row), :].astype(jnp.float32)
        is_lower = lower[r] > 0
        cond = jnp.where(is_lower, mine, other)
        uncond = jnp.where(is_lower, other, mine)
        mix = uncond + scales * (cond - uncond)
        square = jnp.mean(mix * mix, axis=1, keepdims=True)
        buf[r * per_row : (r + 1) * per_row, :] = mix / jnp.sqrt(square + 1e-06)
    for t in range(steps):
        for g in range(share):
            out_ref[t, :, g * HD : (g + 1) * HD] = buf[
                pl.ds(t * share + g, row_dev, stride=per_row), :
            ].astype(jnp.bfloat16)


def shifted(value, axis, steps):
    count = lax.axis_size(axis)
    pairs = [(source, (source + steps) % count) for source in range(count)]
    return lax.ppermute(value, axis, pairs)


def local(
    queries,
    prefix_keys,
    prefix_values,
    suffix_keys,
    suffix_values,
    new_keys,
    new_values,
    lengths,
    pair_of,
    guidance,
):
    steps, row_dev, width = queries.shape
    positions, kv_width = prefix_keys.shape
    kv_heads = kv_width // HD
    heads = width // HD
    group = heads // kv_heads
    suf_dev = suffix_keys.shape[1]
    shards = lax.axis_size("seq")
    share = heads // shards
    rows = steps * row_dev * share
    count = cdiv(rows, HD)
    extra = cdiv(3 * count, 16) * 16
    me = lax.axis_index("seq")

    def meta(dest):
        return jnp.stack([dest, dest * share // group, me * suf_dev]).astype(jnp.int32)

    def partial(dest, own):
        in_specs = [
            pl.BlockSpec((steps, row_dev, share * HD), lambda i, m, n: (0, 0, m[0])),
            pl.BlockSpec((positions, HD), lambda i, m, n: (0, m[1])),
            pl.BlockSpec((positions, HD), lambda i, m, n: (0, m[1])),
            pl.BlockSpec((row_dev, suf_dev, HD), lambda i, m, n: (0, 0, m[1])),
            pl.BlockSpec((row_dev, suf_dev, HD), lambda i, m, n: (0, 0, m[1])),
        ]
        args = [queries, prefix_keys, prefix_values, suffix_keys, suffix_values]
        if own:
            in_specs += [pl.BlockSpec((steps, row_dev, HD), lambda i, m, n: (0, 0, m[1]))] * 2
            args += [new_keys, new_values]
            out_shape = (
                jax.ShapeDtypeStruct((rows, HD), jnp.float32),
                jax.ShapeDtypeStruct((rows, HD), jnp.float32),
            )
            out_specs = (
                pl.BlockSpec((rows, HD), lambda i, m, n: (0, 0)),
                pl.BlockSpec((rows, HD), lambda i, m, n: (0, 0)),
            )
        else:
            out_shape = jax.ShapeDtypeStruct((rows + extra, HD), jnp.bfloat16)
            out_specs = pl.BlockSpec((rows + extra, HD), lambda i, m, n: (0, 0))
        return pl.pallas_call(
            functools.partial(partial_kernel, own, 4),
            grid_spec=pltpu.PrefetchScalarGridSpec(
                num_scalar_prefetch=2,
                grid=(1,),
                in_specs=in_specs,
                out_specs=out_specs,
                scratch_shapes=[
                    pltpu.VMEM((rows, HD), jnp.float32),
                    pltpu.VMEM((count * HD, HD), jnp.float32),
                ],
            ),
            out_shape=out_shape,
            cost_estimate=pl.CostEstimate(
                flops=4 * rows * positions * HD,
                bytes_accessed=4 * positions * HD + 4 * row_dev * suf_dev * HD,
                transcendentals=rows * positions,
            ),
            name="own" if own else "partial",
        )(meta(dest), lengths, *args)

    order = sorted(range(1, shards), key=lambda j: -min(j, shards - j))
    received = []
    for j in order:
        out = partial((me + j) % shards, False)
        received.append(shifted(out, "seq", j))
    own_out, own_lse = partial(me, True)
    attention = pl.pallas_call(
        functools.partial(combine_kernel, shards - 1, rows),
        out_shape=jax.ShapeDtypeStruct((rows, HD), jnp.bfloat16),
        name="combine",
    )(*received, own_out, own_lse)

    mine = lax.axis_index("row") * row_dev + jnp.arange(row_dev, dtype=jnp.int32)
    partner = lax.dynamic_slice_in_dim(pair_of, lax.axis_index("row") * row_dev, row_dev, 0)
    across = shifted(attention, "row", lax.axis_size("row") // 2)
    scales = lax.dynamic_slice_in_dim(guidance, me * share, share, 0)
    aligned = (steps * share) % 16 == 0
    if not aligned:
        across = jnp.take(across.reshape(row_dev, -1, HD), partner % row_dev, axis=0)
        across = across.reshape(rows, HD)
    return pl.pallas_call(
        functools.partial(mix_kernel, aligned),
        grid_spec=pltpu.PrefetchScalarGridSpec(
            num_scalar_prefetch=2,
            grid=(1,),
            in_specs=[
                pl.BlockSpec((rows, HD), lambda i, m, n: (0, 0)),
                pl.BlockSpec((rows, HD), lambda i, m, n: (0, 0)),
                pl.BlockSpec((share, HD), lambda i, m, n: (0, 0)),
            ],
            out_specs=pl.BlockSpec((steps, row_dev, share * HD), lambda i, m, n: (0, 0, 0)),
            scratch_shapes=[pltpu.VMEM((rows, HD), jnp.float32)],
        ),
        out_shape=jax.ShapeDtypeStruct((steps, row_dev, share * HD), jnp.bfloat16),
        name="mix",
    )(
        partner % row_dev,
        (mine < partner).astype(jnp.int32),
        attention,
        across,
        jnp.broadcast_to(scales[:, None], (share, HD)),
    )


def solution(mesh):
    placed = (
        P(None, "row", None),
        P("seq", None),
        P("seq", None),
        P("row", "seq", None),
        P("row", "seq", None),
        P(None, "row", None),
        P(None, "row", None),
        P("row"),
        P(),
        P(),
    )
    return jax.shard_map(
        local, mesh=mesh, in_specs=placed, out_specs=P(None, "row", "seq"), check_vma=False
    )
```

```python
import functools

import jax
import jax.numpy as jnp
from jax import lax
from jax.experimental import pallas as pl
from jax.experimental.pallas import tpu as pltpu
from jax.sharding import PartitionSpec as P

HD = 128
LOG2E = 1.4426950408889634
NEG = -1e30
CHUNK = 4
MIB = 1 << 20
VMEM = pl.BlockSpec(memory_space=pltpu.VMEM)
SMEM = pl.BlockSpec(memory_space=pltpu.SMEM)
HBM = pl.BlockSpec(memory_space=pltpu.HBM)
PIECES = 2


def dot_nt(a, b):
    return lax.dot_general(a, b, (((1,), (1,)), ((), ())), preferred_element_type=jnp.float32)


def dot_nn(a, b):
    return lax.dot_general(a, b, (((1,), (0,)), ((), ())), preferred_element_type=jnp.float32)


def cdiv(a, b):
    return -(-a // b)


def lanes(x):
    return jnp.broadcast_to(x, (x.shape[0], HD))


def with_ones(values):
    return jnp.concatenate([values, jnp.ones_like(values)], axis=1)


def diagonal():
    shape = (HD, HD)
    return lax.broadcasted_iota(jnp.int32, shape, 0) == lax.broadcasted_iota(jnp.int32, shape, 1)


def attend(base, share, lengths, q_ref, k_ref, v_ref, sk_ref, sv_ref, fresh, qs, lses, emit, waits):
    steps, row_dev, _ = q_ref.shape
    per_row = steps * share
    suf_dev = sk_ref.shape[1]
    scale = HD ** (-0.5) * LOG2E
    waits[0]()
    for t in range(steps):
        for g in range(share):
            qs[pl.ds(t * share + g, row_dev, stride=per_row), :] = q_ref[
                t, :, g * HD : (g + 1) * HD
            ].astype(jnp.float32)
    waits[1]()
    keys = k_ref[...]
    size = CHUNK * per_row
    chunks = row_dev // CHUNK

    def scores(c):
        q = qs[c * size : (c + 1) * size, :].astype(jnp.bfloat16)
        parts = [dot_nt(q, keys)]
        suf = []
        for p in range(CHUNK // 2):
            r = c * CHUNK + 2 * p
            sk = sk_ref[r : r + 2].reshape(2 * suf_dev, HD)
            s = dot_nt(q[p * 2 * per_row : (p + 1) * 2 * per_row], sk)
            lane = lax.broadcasted_iota(jnp.int32, s.shape, 1)
            second = lax.broadcasted_iota(jnp.int32, s.shape, 0) >= per_row
            live0 = jnp.clip(lengths[r] - base, 0, suf_dev)
            live1 = jnp.clip(lengths[r + 1] - base, 0, suf_dev)
            low = jnp.where(second, suf_dev, 0)
            high = jnp.where(second, suf_dev + live1, live0)
            suf.append(jnp.where((lane >= low) & (lane < high), s, NEG))
        parts.append(jnp.concatenate(suf, axis=0))
        if fresh is not None:
            s = dot_nt(q, fresh[0])
            row = lax.broadcasted_iota(jnp.int32, s.shape, 0)
            col = lax.broadcasted_iota(jnp.int32, s.shape, 1)
            same = (col % row_dev) == (c * CHUNK + row // per_row)
            causal = (col // row_dev) <= ((row % per_row) // share)
            parts.append(jnp.where(same & causal, s, NEG))
        return parts

    ahead = scores(0)
    waits[2]()
    values = with_ones(v_ref[...])
    for c in range(chunks):
        parts = ahead
        if c + 1 < chunks:
            ahead = scores(c + 1)
        top = jnp.max(parts[0], axis=1, keepdims=True)
        for s in parts[1:]:
            top = jnp.maximum(top, jnp.max(s, axis=1, keepdims=True))
        weights = [jnp.exp2((s - top) * scale).astype(jnp.bfloat16) for s in parts]
        acc = dot_nn(weights[0], values)
        suf = []
        for p in range(CHUNK // 2):
            r = c * CHUNK + 2 * p
            sv = with_ones(sv_ref[r : r + 2].reshape(2 * suf_dev, HD))
            suf.append(dot_nn(weights[1][p * 2 * per_row : (p + 1) * 2 * per_row], sv))
        acc = acc + jnp.concatenate(suf, axis=0)
        if fresh is not None:
            acc = acc + dot_nn(weights[2], fresh[1])
        total = acc[:, HD:]
        part = slice(c * size, (c + 1) * size)
        emit(part, acc[:, :HD] / total)
        lses[part, :] = lanes(top * scale) + jnp.log2(total)


def stat_lines(lses, rows):
    count = cdiv(rows, HD)
    eye = diagonal()
    if count * HD > rows:
        lses[rows:, :] = jnp.zeros((count * HD - rows, HD), jnp.float32)
    lines = [
        jnp.sum(jnp.where(eye, lses[b * HD : (b + 1) * HD, :], 0.0), axis=0, keepdims=True)
        for b in range(count)
    ]
    return jnp.concatenate(lines, axis=0)


def slabs(dest, share, group, state):
    q_ref, k_ref, v_ref, sk_ref, sv_ref = state
    q_at = pl.multiple_of(dest * (share * HD), HD)
    kv_at = pl.multiple_of((dest * share // group) * HD, HD)
    q_lanes, kv_lanes = pl.ds(q_at, share * HD), pl.ds(kv_at, HD)
    return (
        q_ref.at[:, :, q_lanes],
        k_ref.at[:, kv_lanes],
        v_ref.at[:, kv_lanes],
        sk_ref.at[:, :, kv_lanes],
        sv_ref.at[:, :, kv_lanes],
    )


def copies_of(sources, targets, sems):
    out = []
    for i, (source, target) in enumerate(zip(sources, targets)):
        n = source.shape[0]
        pieces = PIECES if i and n % (16 * PIECES) == 0 else 1
        step = n // pieces
        out.append(
            [
                pltpu.make_async_copy(
                    source.at[pl.ds(p * step, step)],
                    target.at[pl.ds(p * step, step)],
                    sems.at[i, p],
                )
                for p in range(pieces)
            ]
        )
    return out


def start(copies):
    for copy in copies:
        copy.start()


def wait(*lists):
    for copies in lists:
        for copy in copies:
            copy.wait()


def send_kernel(share, shifts, group, lengths, *refs):
    state, refs = refs[:5], refs[5:]
    me = lax.axis_index("seq")
    count = lax.axis_size("seq")
    base = me * state[3].shape[1]
    here, later = [lax.rem(me + s, count) for s in shifts]
    now = None
    if len(refs) == 17:
        o_ref, ahead, qs, lses, buffers = refs[0], refs[1:6], refs[6], refs[7], refs[8:13]
        spot, sems, next_sems, spot_sem = refs[13:]
        now = copies_of(slabs(here, share, group, state), buffers, sems)
        size = pltpu.make_async_copy(lengths, spot, spot_sem)
        lengths = spot
        size.start()
        for i in (0, 1, 3, 2, 4):
            start(now[i])
    else:
        buffers, o_ref, ahead, qs, lses, next_sems = refs[:5], refs[5], refs[6:11], refs[11], refs[12], refs[13]
    after = copies_of(slabs(later, share, group, state), ahead, next_sems)

    def fetch():
        for copies in after:
            start(copies)

    if now is None:
        fetch()
        waits = [lambda: None] * 3
    else:

        def wait_keys():
            wait(now[1], now[3])
            size.wait()

        def wait_values():
            wait(now[2], now[4])
            fetch()

        waits = [lambda: wait(now[0]), wait_keys, wait_values]
    rows = qs.shape[0]

    def emit(part, out):
        o_ref[part, :] = out.astype(jnp.bfloat16)

    attend(base, share, lengths, *buffers, None, qs, lses, emit, waits)
    line = stat_lines(lses, rows)
    high = line.astype(jnp.bfloat16).astype(jnp.float32)
    rest = line - high
    middle = rest.astype(jnp.bfloat16).astype(jnp.float32)
    stats = [high, middle, rest - middle]
    pad = o_ref.shape[0] - rows - 3 * line.shape[0]
    if pad:
        stats.append(jnp.zeros((pad, HD), jnp.float32))
    o_ref[rows:, :] = jnp.concatenate(stats, axis=0).astype(jnp.bfloat16)
    wait(*after)


def own_kernel(share, group, lengths, *refs):
    buffers, (nk_ref, nv_ref, o_ref, line_ref, qs, lses) = refs[:5], refs[5:]
    steps, row_dev = nk_ref.shape[:2]
    rows = qs.shape[0]
    me = lax.axis_index("seq")
    kv_lanes = pl.ds(pl.multiple_of((me * share // group) * HD, HD), HD)
    new_keys = nk_ref[:, :, kv_lanes].reshape(steps * row_dev, HD)
    new_values = with_ones(nv_ref[:, :, kv_lanes].reshape(steps * row_dev, HD))

    def emit(part, out):
        o_ref[part, :] = out

    base = me * buffers[3].shape[1]
    waits = [lambda: None] * 3
    attend(base, share, lengths, *buffers, (new_keys, new_values), qs, lses, emit, waits)
    line = stat_lines(lses, rows)
    line_ref[: line.shape[0], :] = line


def combine_kernel(others, *refs):
    received = refs[:others]
    o_ref, line_ref, out_ref = refs[others:]
    rows = o_ref.shape[0]
    count = cdiv(rows, HD)
    lines = [line_ref[:count, :]]
    for ref in received:
        s = ref[rows:, :].astype(jnp.float32)
        lines.append(s[:count] + s[count : 2 * count] + s[2 * count : 3 * count])
    top = functools.reduce(jnp.maximum, lines)
    weights = [jnp.exp2(s - top) for s in lines]
    total = functools.reduce(jnp.add, weights)
    table = jnp.concatenate([w / total for w in weights], axis=0)
    height = cdiv(table.shape[0], HD) * HD
    table = jnp.concatenate([table, jnp.zeros((height - table.shape[0], HD), jnp.float32)], axis=0)
    table = table.T
    for b in range(count):
        size = min(HD, rows - b * HD)
        part = slice(b * HD, b * HD + size)
        acc = o_ref[part, :] * lanes(table[:size, b : b + 1])
        for i, ref in enumerate(received):
            at = (i + 1) * count + b
            acc = acc + ref[part, :].astype(jnp.float32) * lanes(table[:size, at : at + 1])
        out_ref[part, :] = acc.astype(jnp.bfloat16)


def mix_kernel(aligned, pair_of, guidance, a_ref, b_ref, out_ref, buf):
    steps, row_dev, width = out_ref.shape
    share = width // HD
    per_row = steps * share
    head = lax.axis_index("seq") * share
    first = lax.axis_index("row") * row_dev
    index = lax.broadcasted_iota(jnp.int32, (share, HD), 0)
    scales = jnp.zeros((share, HD), jnp.float32)
    for g in range(share):
        scales = jnp.where(index == g, guidance[head + g], scales)
    scales = jnp.concatenate([scales] * steps, axis=0)
    for r in range(row_dev):
        partner = pair_of[first + r]
        mine = a_ref[r * per_row : (r + 1) * per_row, :].astype(jnp.float32)
        if aligned:
            start = pl.multiple_of(lax.rem(partner, row_dev) * per_row, per_row)
        else:
            start = r * per_row
        other = b_ref[pl.ds(start, per_row), :].astype(jnp.float32)
        is_lower = first + r < partner
        cond = jnp.where(is_lower, mine, other)
        uncond = jnp.where(is_lower, other, mine)
        mix = uncond + scales * (cond - uncond)
        square = jnp.mean(mix * mix, axis=1, keepdims=True)
        buf[r * per_row : (r + 1) * per_row, :] = mix / jnp.sqrt(square + 1e-06)
    for t in range(steps):
        for g in range(share):
            out_ref[t, :, g * HD : (g + 1) * HD] = buf[
                pl.ds(t * share + g, row_dev, stride=per_row), :
            ].astype(jnp.bfloat16)


def shifted(value, axis, steps):
    count = lax.axis_size(axis)
    pairs = [(source, (source + steps) % count) for source in range(count)]
    return lax.ppermute(value, axis, pairs)


def local(
    queries,
    prefix_keys,
    prefix_values,
    suffix_keys,
    suffix_values,
    new_keys,
    new_values,
    lengths,
    pair_of,
    guidance,
):
    steps, row_dev, width = queries.shape
    positions, kv_width = prefix_keys.shape
    kv_heads = kv_width // HD
    heads = width // HD
    group = heads // kv_heads
    suf_dev = suffix_keys.shape[1]
    shards = lax.axis_size("seq")
    share = heads // shards
    rows = steps * row_dev * share
    count = cdiv(rows, HD)
    extra = cdiv(3 * count, 16) * 16
    work = [
        pltpu.VMEM((rows, HD), jnp.float32),
        pltpu.VMEM((count * HD, HD), jnp.float32),
    ]
    cost = pl.CostEstimate(
        flops=4 * rows * positions * HD,
        bytes_accessed=4 * positions * HD + 4 * row_dev * suf_dev * HD,
        transcendentals=rows * positions,
    )
    params = pltpu.CompilerParams(vmem_limit_bytes=24 * MIB)
    state = (queries, prefix_keys, prefix_values, suffix_keys, suffix_values)
    state = [pltpu.with_memory_space_constraint(x, pltpu.HBM) for x in state]
    fixed_lengths = pltpu.with_memory_space_constraint(lengths, pltpu.HBM)

    shapes = (
        (steps, row_dev, share * HD),
        (positions, HD),
        (positions, HD),
        (row_dev, suf_dev, HD),
        (row_dev, suf_dev, HD),
    )
    sems = pltpu.SemaphoreType.DMA((5, PIECES))

    def partial(shift, later, operands):
        first = operands is None
        scratch = list(work)
        if first:
            scratch += [pltpu.VMEM(shape, jnp.bfloat16) for shape in shapes]
            scratch += [pltpu.SMEM((row_dev,), jnp.int32), sems]
        scratch.append(sems)
        if first:
            scratch.append(pltpu.SemaphoreType.DMA)
        return pl.pallas_call(
            functools.partial(send_kernel, share, (shift, later), group),
            in_specs=[HBM if first else SMEM] + [HBM] * 5 + ([] if first else [VMEM] * 5),
            out_specs=[VMEM] * 6,
            scratch_shapes=scratch,
            out_shape=[jax.ShapeDtypeStruct((rows + extra, HD), jnp.bfloat16)]
            + [jax.ShapeDtypeStruct(shape, jnp.bfloat16) for shape in shapes],
            cost_estimate=cost,
            compiler_params=params,
            name="partial",
        )(fixed_lengths if first else lengths, *state, *(operands or ()))

    order = sorted(range(1, shards), key=lambda j: -min(j, shards - j))
    received = []
    operands = None
    for j, later in zip(order, order[1:] + [0]):
        out, *operands = partial(j, later, operands)
        received.append(shifted(out, "seq", j))
    own_out, own_line = pl.pallas_call(
        functools.partial(own_kernel, share, group),
        in_specs=[SMEM] + [VMEM] * 7,
        out_specs=(VMEM, VMEM),
        scratch_shapes=work,
        out_shape=(
            jax.ShapeDtypeStruct((rows, HD), jnp.float32),
            jax.ShapeDtypeStruct((cdiv(count, 8) * 8, HD), jnp.float32),
        ),
        cost_estimate=cost,
        compiler_params=params,
        name="own",
    )(lengths, *operands, new_keys, new_values)
    attention = pl.pallas_call(
        functools.partial(combine_kernel, shards - 1),
        in_specs=[VMEM] * (shards + 1),
        out_specs=VMEM,
        out_shape=jax.ShapeDtypeStruct((rows, HD), jnp.bfloat16),
        compiler_params=params,
        name="combine",
    )(*received, own_out, own_line)

    across = shifted(attention, "row", lax.axis_size("row") // 2)
    aligned = (steps * share) % 16 == 0
    if not aligned:
        partner = lax.dynamic_slice_in_dim(pair_of, lax.axis_index("row") * row_dev, row_dev, 0)
        across = jnp.take(across.reshape(row_dev, -1, HD), partner % row_dev, axis=0)
        across = across.reshape(rows, HD)
    return pl.pallas_call(
        functools.partial(mix_kernel, aligned),
        in_specs=[SMEM, SMEM, VMEM, VMEM],
        scratch_shapes=[pltpu.VMEM((rows, HD), jnp.float32)],
        out_specs=VMEM,
        out_shape=jax.ShapeDtypeStruct((steps, row_dev, share * HD), jnp.bfloat16),
        compiler_params=params,
        name="mix",
    )(pair_of, guidance, attention, across)


def solution(mesh):
    placed = (
        P(None, "row", None),
        P("seq", None),
        P("seq", None),
        P("row", "seq", None),
        P("row", "seq", None),
        P(None, "row", None),
        P(None, "row", None),
        P("row"),
        P(),
        P(),
    )
    return jax.shard_map(
        local, mesh=mesh, in_specs=placed, out_specs=P(None, "row", "seq"), check_vma=False
    )
```
